512 devices in a mesh: tensor: 16 (over y, x_hi, core), expert: 32 (over z, x_lo).
Axes of the slice: x: 4 (x_hi: 2, x_lo: 2; x = x_hi * 2 + x_lo), y: 4, z: 16, core: 2. Of those that a mesh axis runs over, the one named last changes fastest.
Arguments:
- tokens_in: bfloat16 [2048, 4096], P('expert', 'tensor'), may hold values from -6 to 6
- residual: bfloat16 [2048, 4096], P('expert', 'tensor'), may hold values from -3 to 3
- w_gate: bfloat16 [32, 4096, 1536], P('expert', 'tensor'), may hold values from -0.09375 to 0.09375
- w_up: bfloat16 [32, 4096, 1536], P('expert', 'tensor'), may hold values from -0.09375 to 0.09375
- w_down: bfloat16 [32, 1536, 4096], P('expert', None, 'tensor'), may hold values from -0.15625 to 0.15625
- expert_ids: int32 [2048, 8], P('expert'), may hold values from 0 to 31, as said below
- slot_pos: int32 [2048, 8], P('expert'), may hold values from 0 to 63, as said below
- route_weights: float32 [2048, 8], P('expert'), may hold values from 0.05 to 0.35
Outputs:
- layer_out: bfloat16 [2048, 4096], P('expert', 'tensor')
The draws below stay inside these ranges and needn't reach their ends.
Inputs may be any that keep to these rules, and one draw needn't show every extreme that they name: `expert_ids`: each row names 8 different experts. `slot_pos`: within each aligned block of 64 rows, the choices that name one expert carry the slots 0, 1, 2 and so on, each once.
All inputs are finite; a program needn't handle non-finite values.
Results may differ from the reference program's by a relative error of at most 0.008.
Values may be sent and summed in bfloat16 or wider, within the bound.
No kernel may reach another device: no remote copies, remote signals or barrier semaphores. Data moves between devices by JAX's collectives and lax.ppermute only.
A program may use at most 64 MiB of HBM per device.

```python
import jax
import jax.numpy as jnp
from jax import lax

D = 4096
EXPERT_HIDDEN = 1536
TOK_E = 64
EXPERTS = 32
TOPK = 8
CAP = 20
TOKENS = 2048
N_EXPERT = 32


def routing_table(key):
    base = jax.random.fold_in(key, 11)
    key_bias, key_noise, key_order, key_hot = jax.random.split(base, 4)
    popular = jax.random.randint(key_bias, (EXPERTS,), 0, 2 ** 14)
    hottest = jax.random.randint(key_hot, (), 0, EXPERTS)
    column = jnp.arange(EXPERTS, dtype=jnp.int32)
    popular = popular + jnp.where(column == hottest, 2 ** 16, 0).astype(jnp.int32)
    noise = jax.random.randint(key_noise, (TOKENS, EXPERTS), 0, 2 ** 15)
    scores = (noise + popular[None, :]) * EXPERTS + column[None, :]
    unused, chosen = lax.top_k(scores, TOPK)
    chosen = chosen.astype(jnp.int32)
    order = jax.random.permutation(key_order, TOKENS * TOPK).astype(jnp.int32)
    block_ids = chosen.reshape(N_EXPERT, TOK_E * TOPK)
    block_order = order.reshape(N_EXPERT, TOK_E * TOPK)
    same = block_ids[:, :, None] == block_ids[:, None, :]
    earlier = block_order[:, None, :] < block_order[:, :, None]
    slots = jnp.sum((same & earlier).astype(jnp.int32), axis=2)
    return (chosen, slots.reshape(TOKENS, TOPK).astype(jnp.int32))


def draw_expert_ids(key, part):
    return routing_table(key)[0]


def draw_slot_pos(key, part):
    return routing_table(key)[1]


def steps_of(rng, extent, pieces, least, high):
    def one(dim, parts):
        steps = jax.random.uniform(jax.random.fold_in(jax.random.fold_in(rng, 6), dim), (parts,), jnp.float32, least / len(pieces), high / len(pieces))
        return jnp.repeat(jnp.exp(steps), extent[dim] // parts).reshape((-1,) + (1,) * (len(extent) - dim - 1))

    level = one(*pieces[0])
    for cut in pieces[1:]:
        level = level * one(*cut)
    return level


def gaussian(own_key, dims, spread, bound, cuts=(), kind=jnp.bfloat16):
    entries = jax.random.normal(own_key, dims, jnp.float32) * spread
    if len(cuts) > 0:
        entries = steps_of(own_key, dims, cuts, -0.22, 0.18) * entries
    return jnp.clip(entries, min=-bound, max=bound).astype(kind)


def setup_inputs(seed: int = 0) -> dict:
    splits = jax.random.split(jax.random.key(seed), 9)
    return {
        "tokens_in": gaussian(splits[0], (TOKENS, D), 1.0, 6.0, ((0, 32), (1, 16))),
        "residual": gaussian(splits[1], (TOKENS, D), 0.5, 3.0, ((0, 32), (1, 16))),
        "w_gate": gaussian(splits[2], (EXPERTS, D, EXPERT_HIDDEN), D ** -0.5, 0.09375, ((0, 32), (1, 16))),
        "w_up": gaussian(splits[3], (EXPERTS, D, EXPERT_HIDDEN), D ** -0.5, 0.09375, ((0, 32), (1, 16))),
        "w_down": gaussian(splits[4], (EXPERTS, EXPERT_HIDDEN, D), EXPERT_HIDDEN ** -0.5, 0.15625, ((0, 32), (2, 16))),
        "expert_ids": draw_expert_ids(jax.random.fold_in(splits[8], 71), 0),
        "slot_pos": draw_slot_pos(jax.random.fold_in(splits[8], 71), 0),
        "route_weights": jnp.clip(0.05 + 0.29999999 * jax.random.uniform(splits[7], (TOKENS, TOPK), jnp.float32) ** steps_of(splits[7], (TOKENS, TOPK), ((0, 32),), -0.2, 0.2), 0.05, 0.35),
    }


def buffer_table(expert_ids, slot_pos):
    tokens = expert_ids.shape[0]
    token_index = jnp.broadcast_to(jnp.arange(tokens, dtype=jnp.int32)[:, None], expert_ids.shape)
    block = token_index // TOK_E
    keep = slot_pos < CAP
    dummy = EXPERTS * N_EXPERT * CAP
    flat = jnp.where(keep, (expert_ids * N_EXPERT + block) * CAP + slot_pos, dummy).astype(jnp.int32)
    table = jnp.full((dummy + 1,), tokens, jnp.int32).at[flat.reshape(-1)].set(token_index.reshape(-1))
    return table[:-1].reshape(EXPERTS, N_EXPERT * CAP), flat


def reference(tokens_in, residual, w_gate, w_up, w_down, expert_ids, slot_pos, route_weights):
    table, flat = buffer_table(expert_ids, slot_pos)
    padded = jnp.concatenate([tokens_in, jnp.zeros((1, D), jnp.bfloat16)], axis=0)
    buffer_rows = N_EXPERT * CAP

    def one_expert(operands):
        index_rows, gate_matrix, up_weight_matrix, down_mat = operands
        token_rows = padded[index_rows]
        gate = jnp.dot(token_rows, gate_matrix, preferred_element_type=jnp.float32)
        up = jnp.dot(token_rows, up_weight_matrix, preferred_element_type=jnp.float32)
        hidden = (jax.nn.silu(gate) * up).astype(jnp.bfloat16)
        return jnp.dot(hidden, down_mat, preferred_element_type=jnp.float32).astype(jnp.bfloat16)

    outputs = lax.map(one_expert, (table, w_gate, w_up, w_down))
    outflat = jnp.concatenate([outputs.reshape(EXPERTS * buffer_rows, D), jnp.zeros((1, D), jnp.bfloat16)], axis=0)
    picked = outflat[flat].astype(jnp.float32)
    mixed = residual.astype(jnp.float32) + jnp.einsum("nk,nkd->nd", route_weights.astype(jnp.float32), picked)
    return mixed.astype(jnp.bfloat16)
```

```python
import functools

import jax
import jax.numpy as jnp
from jax import lax
from jax.experimental import pallas as pl
from jax.experimental.pallas import tpu as pltpu
from jax.sharding import Mesh, PartitionSpec as P

BF = jnp.bfloat16
F32 = jnp.float32
T = ("y", "xh", "c")
R = ("y", "xh")
E = ("z", "xl")
VMEM = pl.BlockSpec(memory_space=pltpu.VMEM)


def call(body, out, *args, name, limit=48 << 20, scratch=(), flops=0, moved=0):
    return pl.pallas_call(
        body,
        out_shape=out,
        in_specs=[VMEM] * len(args),
        out_specs=jax.tree.map(lambda _: VMEM, out),
        scratch_shapes=list(scratch),
        compiler_params=pltpu.CompilerParams(vmem_limit_bytes=limit),
        cost_estimate=pl.CostEstimate(flops=flops, bytes_accessed=moved, transcendentals=0),
        name=name,
    )(*args)


def row_codes(rows):
    r = lax.broadcasted_iota(jnp.int32, (rows, 1), 0)
    base = (r // 8) * 64
    j = lax.rem(r, 8)
    return base + j, base + 8 + j, base + 16 + lax.rem(j, 4), j < 4


def dispatch_body(x_ref, ids_ref, slot_ref, out_ref):
    code = ids_ref[...] * 64 + slot_ref[...]
    x = x_ref[...]
    c0, c1, c2, low = row_codes(out_ref.shape[0])

    def pick(c):
        hit = c == code[0:1, :]
        for k in range(1, code.shape[0]):
            hit = hit | (c == code[k : k + 1, :])
        return jnp.dot(
            jnp.where(hit, 1.0, 0.0).astype(BF), x, preferred_element_type=F32
        )

    out_ref[:, 0:256] = pick(c0).astype(BF)
    out_ref[:, 256:512] = pick(c1).astype(BF)
    tail = pick(c2)
    out_ref[:, 512:640] = jnp.where(low, tail[:, 0:128], tail[:, 128:256]).astype(BF)


def rows_of(a_ref, x_ref):
    n = a_ref.shape[0]
    x_ref[0:n, :] = a_ref[:, 0:256]
    x_ref[n : 2 * n, :] = a_ref[:, 256:512]
    t = a_ref[:, 512:640].astype(F32).reshape(n // 16, 2, 8, 128)
    t0, t1 = t[:, 0], t[:, 1]
    low = lax.broadcasted_iota(jnp.int32, t0.shape, 1) < 4
    b0 = jnp.where(low, t0, pltpu.roll(t1, 4, 1))
    b1 = jnp.where(low, pltpu.roll(t0, 4, 1), t1)
    x_ref[2 * n :, 0:128] = b0.reshape(n // 2, 128).astype(BF)
    x_ref[2 * n :, 128:256] = b1.reshape(n // 2, 128).astype(BF)


def up_body(a_ref, b_ref, wga_ref, wgb_ref, wua_ref, wub_ref, out_ref, xa, xb):
    rows_of(a_ref, xa)
    rows_of(b_ref, xb)
    half = wga_ref.shape[1]

    @pl.loop(0, out_ref.shape[0] // 128)
    def _(i):
        s = pl.ds(pl.multiple_of(i * 128, 128), 128)
        a, b = xa[s, :], xb[s, :]
        for w, v, o in ((wga_ref, wgb_ref, 0), (wua_ref, wub_ref, half)):
            out_ref[s, o : o + half] = (
                jnp.dot(a, w[...], preferred_element_type=F32)
                + jnp.dot(b, v[...], preferred_element_type=F32)
            ).astype(BF)


def act_body(p_ref, h_ref):
    rows = p_ref.shape[0] // 8
    half = h_ref.shape[1]

    @pl.loop(0, rows // 8)
    def _(i):
        def total(o):
            t = None
            for d in range(8):
                v = p_ref[pl.ds(pl.multiple_of(d * rows + i * 8, 8), 8), o : o + half]
                t = v.astype(F32) if t is None else t + v.astype(F32)
            return t

        g, u = total(0), total(half)
        h = (g / (1.0 + jnp.exp(-g)) * u).astype(BF)
        for d in range(8):
            h_ref[pl.ds(pl.multiple_of(d * rows + i * 8, 8), 8), :] = h


def down_body(ha_ref, hb_ref, wa_ref, wb_ref, out_ref):
    n = out_ref.shape[0]

    def rows(s, m):
        return jnp.dot(ha_ref[s : s + m, :], wa_ref[...], preferred_element_type=F32) + jnp.dot(
            hb_ref[s : s + m, :], wb_ref[...], preferred_element_type=F32
        )

    out_ref[:, 0:256] = rows(0, n).astype(BF)
    out_ref[:, 256:512] = rows(n, n).astype(BF)
    t = rows(2 * n, n // 2)
    b0 = t[:, 0:128].reshape(n // 16, 8, 128)
    b1 = t[:, 128:256].reshape(n // 16, 8, 128)
    low = lax.broadcasted_iota(jnp.int32, b0.shape, 1) < 4
    t0 = jnp.where(low, b0, pltpu.roll(b1, 4, 1))
    t1 = jnp.where(low, pltpu.roll(b0, 4, 1), b1)
    out_ref[:, 512:640] = jnp.stack([t0, t1], axis=1).reshape(n, 128).astype(BF)


def combine_body(r_ref, res_ref, ids_ref, slot_ref, w_ref, out_ref):
    code = ids_ref[...] * 64 + slot_ref[...]
    w = w_ref[...]
    c0, c1, c2, low = row_codes(r_ref.shape[0])

    def weights(c):
        t = jnp.where(c == code[0:1, :], w[0:1, :], 0.0)
        for k in range(1, code.shape[0]):
            t = t + jnp.where(c == code[k : k + 1, :], w[k : k + 1, :], 0.0)
        return t

    def mix(m, v):
        hi = m.astype(BF)
        lo = (m - hi.astype(F32)).astype(BF)
        dims = (((0,), (0,)), ((), ()))
        return lax.dot_general(hi, v, dims, preferred_element_type=F32) + lax.dot_general(
            lo, v, dims, preferred_element_type=F32
        )

    total = res_ref[...].astype(F32)
    total += mix(weights(c0), r_ref[:, 0:256]) + mix(weights(c1), r_ref[:, 256:512])
    tail = weights(c2)
    v = r_ref[:, 512:640]
    out_ref[:, 0:128] = (total[:, 0:128] + mix(jnp.where(low, tail, 0.0), v)).astype(BF)
    out_ref[:, 128:256] = (total[:, 128:256] + mix(jnp.where(low, 0.0, tail), v)).astype(BF)


def swap(x):
    return lax.ppermute(x, "c", [(0, 1), (1, 0)])


def spread(x, axes):
    return lax.all_to_all(x, axes, split_axis=0, concat_axis=0, tiled=True)


def shards(tokens_in, residual, w_gate, w_up, w_down, expert_ids, slot_pos, route_weights):
    ids, slots, weights = expert_ids.T, slot_pos.T, route_weights.T
    core = lax.axis_index("c")
    half = w_gate.shape[2] // 2
    sds = jax.ShapeDtypeStruct
    experts = lax.axis_size(E)
    rows = experts * 20

    def halves(w, axis):
        mine = lax.dynamic_slice_in_dim(w, core * half, half, axis)
        other = lax.dynamic_slice_in_dim(w, (1 - core) * half, half, axis)
        return mine, other

    outgoing = call(
        dispatch_body, sds((experts * 8, 640), BF), tokens_in, ids, slots, name="dispatch"
    )
    gate_mine, gate_other = halves(w_gate[0], 1)
    up_mine, up_other = halves(w_up[0], 1)
    gate_recv, up_recv = swap(gate_other), swap(up_other)
    arrived = spread(outgoing, E)
    arrived_b = swap(arrived)
    partial = call(
        up_body,
        sds((rows, 2 * half), BF),
        arrived, arrived_b, gate_mine, gate_recv, up_mine, up_recv,
        scratch=[pltpu.VMEM((rows, 256), BF)] * 2,
        name="gate_up",
    )
    parts = spread(partial, R)
    hidden = call(act_body, sds((rows, half), BF), parts, name="act")
    hidden = spread(hidden, R)
    hidden_b = swap(hidden)
    down_mine, down_other = halves(w_down[0], 0)
    result = call(
        down_body, sds((experts * 8, 640), BF), hidden, hidden_b, down_mine, down_other,
        name="down",
    )
    returned = spread(result, E)
    return call(
        combine_body, sds(tokens_in.shape, BF), returned, residual, ids, slots, weights,
        name="combine",
    )


def solution(mesh):
    fine = Mesh(mesh.devices.reshape(4, 2, 2, 16, 2), T + E)
    in_specs = (
        P(E, T),
        P(E, T),
        P(E, T, None),
        P(E, T, None),
        P(E, None, T),
        P(E, None),
        P(E, None),
        P(E, None),
    )
    return jax.shard_map(
        shards, mesh=fine, in_specs=in_specs, out_specs=P(E, T), check_vma=False
    )
```

```python
import jax
import jax.numpy as jnp
from jax import lax
from jax.experimental import pallas as pl
from jax.experimental.pallas import tpu as pltpu
from jax.sharding import Mesh, PartitionSpec as P

BF = jnp.bfloat16
F32 = jnp.float32
T = ("y", "xh", "c")
E = ("z", "xl")
VMEM = pl.BlockSpec(memory_space=pltpu.VMEM)
HBM = pl.BlockSpec(memory_space=pltpu.HBM)


def call(body, out, *args, name, limit=48 << 20, scratch=(), flops=0, moved=0, stay=()):
    return pl.pallas_call(
        body,
        out_shape=out,
        in_specs=[HBM if i in stay else VMEM for i in range(len(args))],
        out_specs=jax.tree.map(lambda _: HBM if stay else VMEM, out),
        scratch_shapes=list(scratch),
        compiler_params=pltpu.CompilerParams(vmem_limit_bytes=None if stay else limit),
        cost_estimate=pl.CostEstimate(flops=flops, bytes_accessed=moved, transcendentals=0),
        name=name,
    )(*args)


def row_codes(rows, first):
    r = lax.broadcasted_iota(jnp.int32, (rows, 1), 0)
    base = (r // 8) * 64 + first
    j = lax.rem(r, 8)
    return base + j, base + 8 + j // 4, lax.rem(j, 4)


def columns_body(gate_hbm, up_hbm, cols_hbm, sems):
    width, half = cols_hbm.shape[0] // 2, cols_hbm.shape[1] // 2
    core = lax.axis_index("c")
    copies = []
    for k, w in enumerate((gate_hbm, up_hbm)):
        for n, c in enumerate((core, 1 - core)):
            take = pl.ds(pl.multiple_of(c * half, half), half)
            place = cols_hbm.at[n * width : (n + 1) * width, k * half : (k + 1) * half]
            copies.append(pltpu.make_async_copy(w.at[:, take], place, sems.at[2 * k + n]))
    for c in copies:
        c.start()
    for c in copies:
        c.wait()


def dispatch_body(x_ref, y_ref, ids_ref, slot_ref, out_ref):
    code = ids_ref[...] * 64 + slot_ref[...]
    c0, c1, part = row_codes(out_ref.shape[0], 10 * lax.axis_index("xh"))

    def pick(c):
        hit = c == code[0:1, :]
        for k in range(1, code.shape[0]):
            hit = hit | (c == code[k : k + 1, :])
        return jnp.where(hit, 1.0, 0.0).astype(BF)

    def rows(p, ref):
        return jnp.dot(p, ref[...], preferred_element_type=F32)

    p0, p1 = pick(c0), pick(c1)
    out_ref[:, 0:256] = rows(p0, x_ref).astype(BF)
    out_ref[:, 256:512] = rows(p0, y_ref).astype(BF)
    tx, ty = rows(p1, x_ref), rows(p1, y_ref)
    tail = jnp.where(part == 0, tx[:, 0:128], tx[:, 128:256])
    tail2 = jnp.where(part == 2, ty[:, 0:128], ty[:, 128:256])
    out_ref[:, 512:640] = jnp.where(part < 2, tail, tail2).astype(BF)


def rows_of(a_ref, x_ref, t_ref):
    n = a_ref.shape[0]
    x_ref[0:n, :] = a_ref[:, 0:512]
    t_ref[...] = a_ref[:, 512:640].astype(F32)
    for g in range(4):
        x_ref[n:, g * 128 : (g + 1) * 128] = t_ref[pl.ds(g, n // 4, stride=4), :].astype(BF)


def up_body(a_ref, b_ref, waa_ref, wao_ref, wba_ref, wbo_ref, out_ref, xa, xb, ta, tb):
    rows_of(a_ref, xa, ta)
    rows_of(b_ref, xb, tb)

    @pl.loop(0, out_ref.shape[0] // 64)
    def _(i):
        s = pl.ds(pl.multiple_of(i * 64, 64), 64)
        t = None
        for x, w, k in (
            (xa, waa_ref, 0), (xa, wao_ref, 256), (xb, wba_ref, 0), (xb, wbo_ref, 256)
        ):
            v = jnp.dot(x[s, k : k + 256], w[0:256, :], preferred_element_type=F32)
            t = v if t is None else t + v
        out_ref[s, :] = t.astype(BF)


def act_body(p_ref, _, h_ref):
    rows = p_ref.shape[0] // 4
    half = h_ref.shape[1]

    @pl.loop(0, rows // 8)
    def _(i):
        def total(o):
            t = None
            for d in range(4):
                v = p_ref[pl.ds(pl.multiple_of(d * rows + i * 8, 8), 8), o : o + half]
                t = v.astype(F32) if t is None else t + v.astype(F32)
            return t

        g, u = total(0), total(half)
        h = (g / (1.0 + jnp.exp(-g)) * u).astype(BF)
        for d in range(4):
            h_ref[pl.ds(pl.multiple_of(d * rows + i * 8, 8), 8), :] = h


def down_body(ha_ref, hb_ref, w_ref, v0_ref, v1_ref, out_ref, h_ref, t_ref):
    n = out_ref.shape[0]
    half, cut = ha_ref.shape[1], v0_ref.shape[0]
    first = lax.axis_index("c") == 0
    ha, hb = ha_ref[...], hb_ref[...]
    h_ref[:, 0:half] = jnp.where(first, ha, hb)
    h_ref[:, half:] = jnp.where(first, hb, ha)

    def dot(h, m):
        return jnp.dot(h, m, preferred_element_type=F32)

    for k in range(2):
        if k == 0:
            t = dot(h_ref[...], w_ref[...])
        else:
            t = dot(h_ref[:, 0:cut], v0_ref[...]) + dot(h_ref[:, cut:], v1_ref[...])
        out_ref[:, k * 256 : (k + 1) * 256] = t[0:n].astype(BF)
        for g in range(2):
            t_ref[pl.ds(2 * k + g, n // 4, stride=4), :] = t[n:, g * 128 : (g + 1) * 128]
    out_ref[:, 512:640] = t_ref[...].astype(BF)


def combine_body(r_ref, ids_ref, slot_ref, w_ref, own_ref, send_ref):
    code = ids_ref[...] * 64 + slot_ref[...]
    w = w_ref[...]
    c0, c1, part = row_codes(r_ref.shape[0], 10 * lax.axis_index("xh"))

    def weights(c):
        t = jnp.where(c == code[0:1, :], w[0:1, :], 0.0)
        for k in range(1, code.shape[0]):
            t = t + jnp.where(c == code[k : k + 1, :], w[k : k + 1, :], 0.0)
        return t

    def mix(m, v):
        hi = m.astype(BF)
        lo = (m - hi.astype(F32)).astype(BF)
        dims = (((0,), (0,)), ((), ()))
        return lax.dot_general(hi, v, dims, preferred_element_type=F32) + lax.dot_general(
            lo, v, dims, preferred_element_type=F32
        )

    head, tail = weights(c0), weights(c1)
    v = r_ref[:, 512:640]
    for k, ref in ((0, own_ref), (1, send_ref)):
        t = mix(head, r_ref[:, k * 256 : (k + 1) * 256])
        for g in range(2):
            s = slice(g * 128, (g + 1) * 128)
            ref[:, s] = t[:, s] + mix(jnp.where(part == 2 * k + g, tail, 0.0), v)


def finish_body(own_ref, recv_ref, res_ref, out_ref):
    out_ref[...] = (res_ref[...].astype(F32) + own_ref[...] + recv_ref[...]).astype(BF)


def move(x, dx, dc):
    pairs = [(2 * h + c, 2 * ((h + dx) % 2) + (c + dc) % 2) for h in range(2) for c in range(2)]
    return lax.ppermute(x, ("xh", "c"), pairs)


def spread(x, axes):
    return lax.all_to_all(x, axes, split_axis=0, concat_axis=0, tiled=True)


def shards(tokens_in, residual, w_gate, w_up, w_down, expert_ids, slot_pos, route_weights):
    ids, slots, weights = expert_ids.T, slot_pos.T, route_weights.T
    width = tokens_in.shape[1]
    half = w_gate.shape[2] // 2
    sds = jax.ShapeDtypeStruct
    experts = lax.axis_size(E)
    rows = experts * 10
    chunks = sds((experts * 8, 640), BF)

    other_tokens = move(tokens_in, 1, 0)
    cols = call(
        columns_body,
        sds((2 * width, 2 * half), BF),
        w_gate[0], w_up[0],
        scratch=[pltpu.SemaphoreType.DMA((4,))],
        stay=range(2),
        name="columns",
    )
    cols_x = move(cols, 1, 0)
    w_c = move(cols[width:], 0, 1)
    w_xc = move(cols_x[width:], 0, 1)
    cut = half * 2 // 3
    down_first, down_last = move(w_down[0, :cut], 1, 0), move(w_down[0, cut:], 1, 0)
    outgoing = call(
        dispatch_body, chunks, tokens_in, other_tokens, ids, slots, name="dispatch"
    )
    arrived = spread(outgoing, E)
    arrived_b = move(arrived, 0, 1)
    partial = call(
        up_body,
        sds((rows, 2 * half), BF),
        arrived, arrived_b, cols, cols_x, w_c, w_xc,
        scratch=[pltpu.VMEM((rows, 512), BF)] * 2 + [pltpu.VMEM((experts * 8, 128), F32)] * 2,
        name="gate_up",
    )
    parts = spread(partial, "y")
    hidden = call(
        act_body, sds((rows, half), BF), parts, down_first, name="act"
    )
    hidden = spread(hidden, "y")
    hidden_b = move(hidden, 0, 1)
    result = call(
        down_body, chunks, hidden, hidden_b, w_down[0], down_first, down_last,
        scratch=[pltpu.VMEM((rows, 2 * half), BF), pltpu.VMEM((experts * 8, 128), F32)],
        name="down",
    )
    returned = spread(result, E)
    half_out = sds(tokens_in.shape, F32)
    own, send = call(
        combine_body, (half_out, half_out), returned, ids, slots, weights, name="combine"
    )
    recv = move(send, 1, 0)
    return call(finish_body, sds(tokens_in.shape, BF), own, recv, residual, name="finish")


def solution(mesh):
    fine = Mesh(mesh.devices.reshape(4, 2, 2, 16, 2), T + E)
    in_specs = (
        P(E, T),
        P(E, T),
        P(E, T, None),
        P(E, T, None),
        P(E, None, T),
        P(E, None),
        P(E, None),
        P(E, None),
    )
    return jax.shard_map(
        shards, mesh=fine, in_specs=in_specs, out_specs=P(E, T), check_vma=False
    )
```

```python
import jax
import jax.numpy as jnp
from jax import lax
from jax.experimental import pallas as pl
from jax.experimental.pallas import tpu as pltpu
from jax.sharding import Mesh, PartitionSpec as P

BF = jnp.bfloat16
F32 = jnp.float32
T = ("y", "xh", "c")
R = ("y", "xh")
E = ("z", "xl")
VMEM = pl.BlockSpec(memory_space=pltpu.VMEM)
HBM = pl.BlockSpec(memory_space=pltpu.HBM)


def call(body, out, *args, name, limit=48 << 20, scratch=(), flops=0, moved=0, stay=()):
    return pl.pallas_call(
        body,
        out_shape=out,
        in_specs=[HBM if i in stay else VMEM for i in range(len(args))],
        out_specs=jax.tree.map(lambda _: VMEM, out),
        scratch_shapes=list(scratch),
        compiler_params=pltpu.CompilerParams(vmem_limit_bytes=None if stay else limit),
        cost_estimate=pl.CostEstimate(flops=flops, bytes_accessed=moved, transcendentals=0),
        name=name,
    )(*args)


def row_codes(rows):
    r = lax.broadcasted_iota(jnp.int32, (rows, 1), 0)
    base = (r // 8) * 64
    j = lax.rem(r, 8)
    return base + j, base + 8 + j, base + 16 + lax.rem(j, 4), j < 4


def dispatch_body(x_hbm, ids_hbm, slot_hbm, out_ref, x_ref, ids_ref, slot_ref, sems):
    copies = [
        pltpu.make_async_copy(a, b, sems.at[i])
        for i, (a, b) in enumerate(((ids_hbm, ids_ref), (slot_hbm, slot_ref), (x_hbm, x_ref)))
    ]
    for c in copies:
        c.start()
    c0, c1, c2, low = row_codes(out_ref.shape[0])
    for c in copies:
        c.wait()
    code = ids_ref[...] * 64 + slot_ref[...]
    x = x_ref[...]

    def pick(c):
        hit = c == code[0:1, :]
        for k in range(1, code.shape[0]):
            hit = hit | (c == code[k : k + 1, :])
        return jnp.dot(
            jnp.where(hit, 1.0, 0.0).astype(BF), x, preferred_element_type=F32
        )

    out_ref[:, 0:256] = pick(c0).astype(BF)
    out_ref[:, 256:512] = pick(c1).astype(BF)
    tail = pick(c2)
    out_ref[:, 512:640] = jnp.where(low, tail[:, 0:128], tail[:, 128:256]).astype(BF)


def rows_of(a_ref, x_ref):
    n = a_ref.shape[0]
    x_ref[0:n, :] = a_ref[:, 0:256]
    x_ref[n : 2 * n, :] = a_ref[:, 256:512]
    t = a_ref[:, 512:640].astype(F32).reshape(n // 16, 2, 8, 128)
    t0, t1 = t[:, 0], t[:, 1]
    low = lax.broadcasted_iota(jnp.int32, t0.shape, 1) < 4
    b0 = jnp.where(low, t0, pltpu.roll(t1, 4, 1))
    b1 = jnp.where(low, pltpu.roll(t0, 4, 1), t1)
    x_ref[2 * n :, 0:128] = b0.reshape(n // 2, 128).astype(BF)
    x_ref[2 * n :, 128:256] = b1.reshape(n // 2, 128).astype(BF)


def up_body(x_ref, wga_ref, wgb_ref, wua_ref, wub_ref, _, out_ref, xa, xb):
    n = x_ref.shape[0] // 2
    core = lax.axis_index("c")
    rows_of(x_ref.at[pl.ds(pl.multiple_of(core * n, n), n)], xa)
    rows_of(x_ref.at[pl.ds(pl.multiple_of((1 - core) * n, n), n)], xb)
    half = wga_ref.shape[1]

    @pl.loop(0, out_ref.shape[0] // 128)
    def _(i):
        s = pl.ds(pl.multiple_of(i * 128, 128), 128)
        a, b = xa[s, :], xb[s, :]
        for w, v, o in ((wga_ref, wgb_ref, 0), (wua_ref, wub_ref, half)):
            out_ref[s, o : o + half] = (
                jnp.dot(a, w[...], preferred_element_type=F32)
                + jnp.dot(b, v[...], preferred_element_type=F32)
            ).astype(BF)


def act_body(p_ref, h_ref):
    rows = p_ref.shape[0] // 8
    half = h_ref.shape[1]

    @pl.loop(0, rows // 8)
    def _(i):
        def total(o):
            t = None
            for d in range(8):
                v = p_ref[pl.ds(pl.multiple_of(d * rows + i * 8, 8), 8), o : o + half]
                t = v.astype(F32) if t is None else t + v.astype(F32)
            return t

        g, u = total(0), total(half)
        h = (g / (1.0 + jnp.exp(-g)) * u).astype(BF)
        for d in range(8):
            h_ref[pl.ds(pl.multiple_of(d * rows + i * 8, 8), 8), :] = h


def down_body(ha_ref, hb_ref, wa_ref, wb_ref, out_ref):
    n = out_ref.shape[0]

    def rows(s, m):
        return jnp.dot(ha_ref[s : s + m, :], wa_ref[...], preferred_element_type=F32) + jnp.dot(
            hb_ref[s : s + m, :], wb_ref[...], preferred_element_type=F32
        )

    out_ref[:, 0:256] = rows(0, n).astype(BF)
    out_ref[:, 256:512] = rows(n, n).astype(BF)
    t = rows(2 * n, n // 2)
    b0 = t[:, 0:128].reshape(n // 16, 8, 128)
    b1 = t[:, 128:256].reshape(n // 16, 8, 128)
    low = lax.broadcasted_iota(jnp.int32, b0.shape, 1) < 4
    t0 = jnp.where(low, b0, pltpu.roll(b1, 4, 1))
    t1 = jnp.where(low, pltpu.roll(b0, 4, 1), b1)
    out_ref[:, 512:640] = jnp.stack([t0, t1], axis=1).reshape(n, 128).astype(BF)


def weigh_body(ids_ref, slot_ref, w_ref, out_ref):
    code = ids_ref[...] * 64 + slot_ref[...]
    w = w_ref[...]
    rows = out_ref.shape[1]
    c0, c1, c2, low = row_codes(rows)

    def weights(c):
        t = jnp.where(c == code[0:1, :], w[0:1, :], 0.0)
        for k in range(1, code.shape[0]):
            t = t + jnp.where(c == code[k : k + 1, :], w[k : k + 1, :], 0.0)
        return t

    tail = weights(c2)
    sets = (weights(c0), weights(c1), jnp.where(low, tail, 0.0), jnp.where(low, 0.0, tail))
    for k, m in enumerate(sets):
        m = jnp.transpose(m)
        hi = m.astype(BF)
        n = m.shape[0]
        out_ref[2 * k * n : (2 * k + 1) * n, :] = hi
        out_ref[(2 * k + 1) * n : (2 * k + 2) * n, :] = (m - hi.astype(F32)).astype(BF)


def combine_body(r_ref, res_ref, m_ref, out_ref):
    n = res_ref.shape[0]

    def mix(k, v):
        t = jnp.dot(m_ref[2 * k * n : (2 * k + 2) * n, :], v, preferred_element_type=F32)
        return t[0:n] + t[n:]

    total = res_ref[...].astype(F32) + mix(0, r_ref[:, 0:256]) + mix(1, r_ref[:, 256:512])
    v = r_ref[:, 512:640]
    out_ref[:, 0:128] = (total[:, 0:128] + mix(2, v)).astype(BF)
    out_ref[:, 128:256] = (total[:, 128:256] + mix(3, v)).astype(BF)


def swap(x):
    return lax.ppermute(x, "c", [(0, 1), (1, 0)])


def spread(x, axes):
    return lax.all_to_all(x, axes, split_axis=0, concat_axis=0, tiled=True)


def shards(tokens_in, residual, w_gate, w_up, w_down, expert_ids, slot_pos, route_weights):
    ids, slots, weights = expert_ids.T, slot_pos.T, route_weights.T
    core = lax.axis_index("c")
    half = w_gate.shape[2] // 2
    sds = jax.ShapeDtypeStruct
    experts = lax.axis_size(E)
    rows = experts * 20

    def halves(w, axis):
        mine = lax.dynamic_slice_in_dim(w, core * half, half, axis)
        other = lax.dynamic_slice_in_dim(w, (1 - core) * half, half, axis)
        return mine, other

    outgoing = call(
        dispatch_body, sds((experts * 8, 640), BF), tokens_in, ids, slots,
        scratch=[
            pltpu.VMEM(tokens_in.shape, BF),
            pltpu.VMEM(ids.shape, jnp.int32),
            pltpu.VMEM(ids.shape, jnp.int32),
            pltpu.SemaphoreType.DMA((3,)),
        ],
        stay=range(3),
        name="dispatch",
    )
    mixing = call(
        weigh_body, sds((8 * ids.shape[1], experts * 8), BF), ids, slots, weights, name="weigh"
    )
    gate_mine, gate_other = halves(w_gate[0], 1)
    up_mine, up_other = halves(w_up[0], 1)
    gate_recv, up_recv = swap(gate_other), swap(up_other)
    arrived = spread(outgoing, E)
    arrived = lax.all_gather(arrived, "c", axis=0, tiled=True)
    partial = call(
        up_body,
        sds((rows, 2 * half), BF),
        arrived, gate_mine, gate_recv, up_mine, up_recv, mixing,
        scratch=[pltpu.VMEM((rows, 256), BF)] * 2,
        name="gate_up",
    )
    parts = spread(partial, R)
    hidden = call(act_body, sds((rows, half), BF), parts, name="act")
    hidden = spread(hidden, R)
    hidden_b = swap(hidden)
    down_mine, down_other = halves(w_down[0], 0)
    result = call(
        down_body, sds((experts * 8, 640), BF), hidden, hidden_b, down_mine, down_other,
        name="down",
    )
    returned = spread(result, E)
    return call(
        combine_body, sds(tokens_in.shape, BF), returned, residual, mixing, name="combine"
    )


def solution(mesh):
    fine = Mesh(mesh.devices.reshape(4, 2, 2, 16, 2), T + E)
    in_specs = (
        P(E, T),
        P(E, T),
        P(E, T, None),
        P(E, T, None),
        P(E, None, T),
        P(E, None),
        P(E, None),
        P(E, None),
    )
    return jax.shard_map(
        shards, mesh=fine, in_specs=in_specs, out_specs=P(E, T), check_vma=False
    )
```

```python
import jax
import jax.numpy as jnp
from jax import lax
from jax.experimental import pallas as pl
from jax.experimental.pallas import tpu as pltpu
from jax.sharding import Mesh, PartitionSpec as P

BF = jnp.bfloat16
F32 = jnp.float32
T = ("y", "xh", "c")
R = ("y", "xh")
E = ("z", "xl")
LINE = ("xl", "z")
VMEM = pl.BlockSpec(memory_space=pltpu.VMEM)
HBM = pl.BlockSpec(memory_space=pltpu.HBM)


def call(body, out, *args, name, limit=16 << 20, scratch=(), stay=False):
    return pl.pallas_call(
        body,
        out_shape=out,
        in_specs=[HBM if stay else VMEM] * len(args),
        out_specs=jax.tree.map(lambda _: VMEM, out),
        scratch_shapes=list(scratch),
        compiler_params=pltpu.CompilerParams(vmem_limit_bytes=None if stay else limit),
        name=name,
    )(*args)


def row_codes(rows, first):
    r = lax.broadcasted_iota(jnp.int32, (rows, 1), 0)
    d, j = r // 8, lax.rem(r, 8)
    experts = rows // 8
    base = (lax.rem(d, experts // 2) * 2 + d // (experts // 2)) * 64 + first
    return base + j, base + 8 + j // 4, lax.rem(j, 4)


def part_of(ref, index, count):
    return ref[pl.ds(pl.multiple_of(index * count, count), count), :]


def dispatch_body(x_hbm, ids_hbm, slot_hbm, out_ref, x_ref, ids_ref, slot_ref, sems):
    copies = [
        pltpu.make_async_copy(a, b, sems.at[i])
        for i, (a, b) in enumerate(((ids_hbm, ids_ref), (slot_hbm, slot_ref), (x_hbm, x_ref)))
    ]
    for c in copies:
        c.start()
    core = lax.axis_index("c")
    n = x_ref.shape[0] // 2
    c0, c1, part = row_codes(out_ref.shape[0], 10 * core)
    for c in copies:
        c.wait()
    code = ids_ref[...] * 64 + slot_ref[...]
    own, other = part_of(x_ref, core, n), part_of(x_ref, 1 - core, n)

    def pick(c):
        hit = c == code[0:1, :]
        for k in range(1, code.shape[0]):
            hit = hit | (c == code[k : k + 1, :])
        return jnp.where(hit, 1.0, 0.0).astype(BF)

    def rows(p, x):
        return jnp.dot(p, x, preferred_element_type=F32)

    p0, p1 = pick(c0), pick(c1)
    out_ref[:, 0:256] = rows(p0, own).astype(BF)
    out_ref[:, 256:512] = rows(p0, other).astype(BF)
    tx, ty = rows(p1, own), rows(p1, other)
    tail = jnp.where(part == 0, tx[:, 0:128], tx[:, 128:256])
    tail2 = jnp.where(part == 2, ty[:, 0:128], ty[:, 128:256])
    out_ref[:, 512:640] = jnp.where(part < 2, tail, tail2).astype(BF)


def stack_body(ga_ref, gb_ref, ua_ref, ub_ref, _, __, out_ref):
    k, half = ga_ref.shape
    out_ref[0:k, 0:half] = ga_ref[...]
    out_ref[k:, 0:half] = gb_ref[...]
    out_ref[0:k, half:] = ua_ref[...]
    out_ref[k:, half:] = ub_ref[...]


def up_body(a_ref, w_ref, out_ref, x_ref, t_ref):
    n = a_ref.shape[0]
    x_ref[0:n, :] = a_ref[:, 0:512]
    t_ref[...] = a_ref[:, 512:640].astype(F32)
    for g in range(4):
        x_ref[n:, g * 128 : (g + 1) * 128] = t_ref[pl.ds(g, n // 4, stride=4), :].astype(BF)

    @pl.loop(0, out_ref.shape[0] // 64)
    def _(i):
        s = pl.ds(pl.multiple_of(i * 64, 64), 64)
        out_ref[s, :] = jnp.dot(x_ref[s, :], w_ref[...], preferred_element_type=F32).astype(BF)


def act_body(p_ref, h_ref):
    rows = p_ref.shape[0] // 8
    half = h_ref.shape[1]

    @pl.loop(0, rows // 8)
    def _(i):
        def total(o):
            t = None
            for d in range(8):
                v = p_ref[pl.ds(pl.multiple_of(d * rows + i * 8, 8), 8), o : o + half]
                t = v.astype(F32) if t is None else t + v.astype(F32)
            return t

        g, u = total(0), total(half)
        h = (g / (1.0 + jnp.exp(-g)) * u).astype(BF)
        for d in range(8):
            h_ref[pl.ds(pl.multiple_of(d * rows + i * 8, 8), 8), :] = h


def down_body(h_ref, w_ref, v_ref, out_ref, t_ref):
    n = out_ref.shape[0]
    for k, m in ((0, w_ref), (1, v_ref)):
        t = jnp.dot(h_ref[...], m[...], preferred_element_type=F32)
        out_ref[:, k * 256 : (k + 1) * 256] = t[0:n].astype(BF)
        for g in range(2):
            t_ref[pl.ds(2 * k + g, n // 4, stride=4), :] = t[n:, g * 128 : (g + 1) * 128]
    out_ref[:, 512:640] = t_ref[...].astype(BF)


def weigh_body(ids_ref, slot_ref, w_ref, out_ref):
    code = ids_ref[...] * 64 + slot_ref[...]
    w = w_ref[...]
    c0, c1, part = row_codes(out_ref.shape[1], 10 * lax.axis_index("c"))

    def weights(c):
        t = jnp.where(c == code[0:1, :], w[0:1, :], 0.0)
        for k in range(1, code.shape[0]):
            t = t + jnp.where(c == code[k : k + 1, :], w[k : k + 1, :], 0.0)
        return t

    tail = weights(c1)
    sets = [weights(c0)] + [jnp.where(part == p, tail, 0.0) for p in range(4)]
    for k, m in enumerate(sets):
        m = jnp.transpose(m)
        hi = m.astype(BF)
        n = m.shape[0]
        out_ref[2 * k * n : (2 * k + 1) * n, :] = hi
        out_ref[(2 * k + 1) * n : (2 * k + 2) * n, :] = (m - hi.astype(F32)).astype(BF)


def combine_body(r_ref, m_ref, own_ref, send_ref):
    n = own_ref.shape[0]
    head = jnp.dot(m_ref[0 : 2 * n, :], r_ref[:, 0:512], preferred_element_type=F32)
    head = head[0:n] + head[n:]
    tail = jnp.dot(m_ref[2 * n :, :], r_ref[:, 512:640], preferred_element_type=F32)
    for k, ref in ((0, own_ref), (1, send_ref)):
        for g in range(2):
            p = 2 * k + g
            s = tail[2 * p * n : (2 * p + 1) * n] + tail[(2 * p + 1) * n : (2 * p + 2) * n]
            ref[:, g * 128 : (g + 1) * 128] = head[:, p * 128 : (p + 1) * 128] + s


def finish_body(own_ref, sent_ref, res_ref, out_ref):
    other = part_of(sent_ref, 1 - lax.axis_index("c"), own_ref.shape[0])
    out_ref[...] = (res_ref[...].astype(F32) + own_ref[...] + other).astype(BF)


def swap(x):
    return lax.ppermute(x, "c", [(0, 1), (1, 0)])


def share(x):
    return lax.all_gather(x, "c", axis=0, tiled=True)


def spread(x, axes):
    return lax.all_to_all(x, axes, split_axis=0, concat_axis=0, tiled=True)


def shards(tokens_in, residual, w_gate, w_up, w_down, expert_ids, slot_pos, route_weights):
    ids, slots, weights = expert_ids.T, slot_pos.T, route_weights.T
    hidden_units = w_gate.shape[2]
    sds = jax.ShapeDtypeStruct
    experts = lax.axis_size(E)
    rows = experts * 10
    chunks = sds((experts * 8, 640), BF)
    gate, up, down = w_gate[0], w_up[0], w_down[0]

    tokens = share(tokens_in)
    outgoing = call(
        dispatch_body, chunks, tokens, ids, slots,
        scratch=[
            pltpu.VMEM(tokens.shape, BF),
            pltpu.VMEM(ids.shape, jnp.int32),
            pltpu.VMEM(ids.shape, jnp.int32),
            pltpu.SemaphoreType.DMA((3,)),
        ],
        stay=True,
        name="dispatch",
    )
    mixing = call(
        weigh_body, sds((10 * ids.shape[1], experts * 8), BF), ids, slots, weights, name="weigh"
    )
    gate_b, up_b, down_b = swap(gate), swap(up), swap(down)
    stacked = call(
        stack_body, sds((2 * gate.shape[0], 2 * hidden_units), BF),
        gate, gate_b, up, up_b, down_b, mixing,
        name="stack",
    )
    arrived = spread(outgoing, LINE)
    partial = call(
        up_body,
        sds((rows, 2 * hidden_units), BF),
        arrived, stacked,
        scratch=[pltpu.VMEM((rows, 512), BF), pltpu.VMEM((experts * 8, 128), F32)],
        name="gate_up",
    )
    parts = spread(partial, R)
    hidden = call(act_body, sds((rows, hidden_units), BF), parts, name="act")
    hidden = spread(hidden, R)
    result = call(
        down_body, chunks, hidden, down, down_b,
        scratch=[pltpu.VMEM((experts * 8, 128), F32)],
        name="down",
    )
    returned = spread(result, LINE)
    half_out = sds(tokens_in.shape, F32)
    own, send = call(combine_body, (half_out, half_out), returned, mixing, name="combine")
    return call(
        finish_body, sds(tokens_in.shape, BF), own, share(send), residual, name="finish"
    )


def solution(mesh):
    fine = Mesh(mesh.devices.reshape(4, 2, 2, 16, 2), T + E)
    in_specs = (
        P(E, T),
        P(E, T),
        P(E, T, None),
        P(E, T, None),
        P(E, None, T),
        P(E, None),
        P(E, None),
        P(E, None),
    )
    return jax.shard_map(
        shards, mesh=fine, in_specs=in_specs, out_specs=P(E, T), check_vma=False
    )
```

```python
import jax
import jax.numpy as jnp
from jax import lax
from jax.experimental import pallas as pl
from jax.experimental.pallas import tpu as pltpu
from jax.sharding import Mesh, PartitionSpec as P

BF = jnp.bfloat16
F32 = jnp.float32
T = ("y", "xh", "c")
R = ("y", "xh")
E = ("z", "xl")
LINE = ("xl", "z")
VMEM = pl.BlockSpec(memory_space=pltpu.VMEM)


def call(body, out, *args, name, limit=16 << 20, scratch=()):
    return pl.pallas_call(
        body,
        out_shape=out,
        in_specs=[VMEM] * len(args),
        out_specs=jax.tree.map(lambda _: VMEM, out),
        scratch_shapes=list(scratch),
        compiler_params=pltpu.CompilerParams(vmem_limit_bytes=limit),
        name=name,
    )(*args)


def row_codes(rows, first):
    r = lax.broadcasted_iota(jnp.int32, (rows, 1), 0)
    d, j = r // 8, lax.rem(r, 8)
    experts = rows // 8
    base = (lax.rem(d, experts // 2) * 2 + d // (experts // 2)) * 64 + first
    return base + j, base + 8 + j // 4, lax.rem(j, 4)


def part_of(ref, index, count):
    return ref[pl.ds(pl.multiple_of(index * count, count), count), :]


def dispatch_body(x_ref, code_ref, out_ref):
    core = lax.axis_index("c")
    n = x_ref.shape[0] // 2
    c0, c1, part = row_codes(out_ref.shape[0], 10 * core)
    code = code_ref[...]
    own, other = part_of(x_ref, core, n), part_of(x_ref, 1 - core, n)

    def pick(c):
        hit = c == code[0:1, :]
        for k in range(1, code.shape[0]):
            hit = hit | (c == code[k : k + 1, :])
        return jnp.where(hit, 1.0, 0.0).astype(BF)

    def rows(p, x):
        return jnp.dot(p, x, preferred_element_type=F32)

    p0, p1 = pick(c0), pick(c1)
    out_ref[:, 0:256] = rows(p0, own).astype(BF)
    out_ref[:, 256:512] = rows(p0, other).astype(BF)
    tx, ty = rows(p1, own), rows(p1, other)
    tail = jnp.where(part == 0, tx[:, 0:128], tx[:, 128:256])
    tail2 = jnp.where(part == 2, ty[:, 0:128], ty[:, 128:256])
    out_ref[:, 512:640] = jnp.where(part < 2, tail, tail2).astype(BF)


def stack_body(ga_ref, gb_ref, ua_ref, ub_ref, _, __, out_ref):
    k, half = ga_ref.shape
    out_ref[0:k, 0:half] = ga_ref[...]
    out_ref[k:, 0:half] = gb_ref[...]
    out_ref[0:k, half:] = ua_ref[...]
    out_ref[k:, half:] = ub_ref[...]


def up_body(a_ref, w_ref, out_ref, x_ref, t_ref):
    n = a_ref.shape[0]
    x_ref[0:n, :] = a_ref[:, 0:512]
    t_ref[...] = a_ref[:, 512:640].astype(F32)
    for g in range(4):
        x_ref[n:, g * 128 : (g + 1) * 128] = t_ref[pl.ds(g, n // 4, stride=4), :].astype(BF)

    out_ref[...] = jnp.dot(x_ref[...], w_ref[...], preferred_element_type=F32).astype(BF)


def act_body(p_ref, h_ref):
    rows = p_ref.shape[0] // 8
    half = h_ref.shape[1]

    @pl.loop(0, rows // 8)
    def _(i):
        def total(o):
            t = None
            for d in range(8):
                v = p_ref[pl.ds(pl.multiple_of(d * rows + i * 8, 8), 8), o : o + half]
                t = v.astype(F32) if t is None else t + v.astype(F32)
            return t

        g, u = total(0), total(half)
        h = (g / (1.0 + jnp.exp(-g)) * u).astype(BF)
        for d in range(8):
            h_ref[pl.ds(pl.multiple_of(d * rows + i * 8, 8), 8), :] = h


def down_body(h_ref, w_ref, v_ref, out_ref, t_ref):
    n = out_ref.shape[0]
    for k, m in ((0, w_ref), (1, v_ref)):
        t = jnp.dot(h_ref[...], m[...], preferred_element_type=F32)
        out_ref[:, k * 256 : (k + 1) * 256] = t[0:n].astype(BF)
        for g in range(2):
            t_ref[pl.ds(2 * k + g, n // 4, stride=4), :] = t[n:, g * 128 : (g + 1) * 128]
    out_ref[:, 512:640] = t_ref[...].astype(BF)


def weigh_body(code_ref, w_ref, out_ref):
    code = code_ref[...]
    w = w_ref[...]
    c0, c1, _ = row_codes(out_ref.shape[1], 10 * lax.axis_index("c"))

    def weights(c):
        t = jnp.where(c == code[0:1, :], w[0:1, :], 0.0)
        for k in range(1, code.shape[0]):
            t = t + jnp.where(c == code[k : k + 1, :], w[k : k + 1, :], 0.0)
        return t

    for k, m in enumerate((weights(c0), weights(c1))):
        m = jnp.transpose(m)
        hi = m.astype(BF)
        n = m.shape[0]
        out_ref[2 * k * n : (2 * k + 1) * n, :] = hi
        out_ref[(2 * k + 1) * n : (2 * k + 2) * n, :] = (m - hi.astype(F32)).astype(BF)


def combine_body(r_ref, m_ref, own_ref, send_ref):
    n = own_ref.shape[0]
    head = jnp.dot(m_ref[0 : 2 * n, :], r_ref[:, 0:512], preferred_element_type=F32)
    head = head[0:n] + head[n:]
    rest = r_ref[:, 512:640]
    part = lax.rem(lax.broadcasted_iota(jnp.int32, rest.shape, 0), 4)
    parts = [jnp.where(part == p, rest, 0.0).astype(BF) for p in range(4)]
    tail = jnp.dot(m_ref[2 * n :, :], jnp.concatenate(parts, axis=1), preferred_element_type=F32)
    for k, ref in ((0, own_ref), (1, send_ref)):
        for g in range(2):
            p = 2 * k + g
            s = slice(p * 128, (p + 1) * 128)
            ref[:, g * 128 : (g + 1) * 128] = head[:, s] + tail[0:n, s] + tail[n:, s]


def finish_body(own_ref, sent_ref, res_ref, out_ref):
    other = part_of(sent_ref, 1 - lax.axis_index("c"), own_ref.shape[0])
    out_ref[...] = (res_ref[...].astype(F32) + own_ref[...] + other).astype(BF)


def swap(x):
    return lax.ppermute(x, "c", [(0, 1), (1, 0)])


def share(x):
    return lax.all_gather(x, "c", axis=0, tiled=True)


def spread(x, axes):
    return lax.all_to_all(x, axes, split_axis=0, concat_axis=0, tiled=True)


def shards(tokens_in, residual, w_gate, w_up, w_down, expert_ids, slot_pos, route_weights):
    code, weights = (expert_ids * 64 + slot_pos).T, route_weights.T
    hidden_units = w_gate.shape[2]
    sds = jax.ShapeDtypeStruct
    experts = lax.axis_size(E)
    rows = experts * 10
    chunks = sds((experts * 8, 640), BF)
    gate, up, down = w_gate[0], w_up[0], w_down[0]

    tokens = share(tokens_in)
    outgoing = call(dispatch_body, chunks, tokens, code, name="dispatch")
    mixing = call(
        weigh_body, sds((4 * code.shape[1], experts * 8), BF), code, weights, name="weigh"
    )
    gate_b, up_b, down_b = swap(gate), swap(up), swap(down)
    stacked = call(
        stack_body, sds((2 * gate.shape[0], 2 * hidden_units), BF),
        gate, gate_b, up, up_b, down_b, mixing,
        name="stack",
    )
    arrived = spread(outgoing, LINE)
    partial = call(
        up_body,
        sds((rows, 2 * hidden_units), BF),
        arrived, stacked,
        scratch=[pltpu.VMEM((rows, 512), BF), pltpu.VMEM((experts * 8, 128), F32)],
        name="gate_up",
    )
    parts = spread(partial, R)
    hidden = call(act_body, sds((rows, hidden_units), BF), parts, name="act")
    hidden = spread(hidden, R)
    result = call(
        down_body, chunks, hidden, down, down_b,
        scratch=[pltpu.VMEM((experts * 8, 128), F32)],
        name="down",
    )
    returned = spread(result, LINE)
    half_out = sds(tokens_in.shape, F32)
    own, send = call(combine_body, (half_out, half_out), returned, mixing, name="combine")
    return call(
        finish_body, sds(tokens_in.shape, BF), own, share(send), residual, name="finish"
    )


def solution(mesh):
    fine = Mesh(mesh.devices.reshape(4, 2, 2, 16, 2), T + E)
    in_specs = (
        P(E, T),
        P(E, T),
        P(E, T, None),
        P(E, T, None),
        P(E, None, T),
        P(E, None),
        P(E, None),
        P(E, None),
    )
    return jax.shard_map(
        shards, mesh=fine, in_specs=in_specs, out_specs=P(E, T), check_vma=False
    )
```

```python
import jax
import jax.numpy as jnp
from jax import lax
from jax.experimental import pallas as pl
from jax.experimental.pallas import tpu as pltpu
from jax.sharding import Mesh, PartitionSpec as P

BF = jnp.bfloat16
F32 = jnp.float32
T = ("y", "xh", "c")
R = ("y", "xh")
E = ("za", "zb", "xl")
LINE = ("xl", "zb", "za")
VMEM = pl.BlockSpec(memory_space=pltpu.VMEM)


def call(body, out, *args, name, limit=16 << 20, scratch=()):
    return pl.pallas_call(
        body,
        out_shape=out,
        in_specs=[VMEM] * len(args),
        out_specs=jax.tree.map(lambda _: VMEM, out),
        scratch_shapes=list(scratch),
        compiler_params=pltpu.CompilerParams(vmem_limit_bytes=limit),
        name=name,
    )(*args)


def expert_of(chunk):
    total, left = 0, chunk
    for axis in reversed(LINE):
        size = lax.axis_size(axis)
        stride = lax.axis_size(E[E.index(axis) + 1 :]) if axis != E[-1] else 1
        total = total + lax.rem(left, size) * stride
        left = left // size
    return total


def row_codes(rows, first):
    r = lax.broadcasted_iota(jnp.int32, (rows, 1), 0)
    d, j = r // 8, lax.rem(r, 8)
    base = expert_of(d) * 64 + first
    return base + j, base + 8 + j // 4, lax.rem(j, 4)


def part_of(ref, index, count):
    return ref[pl.ds(pl.multiple_of(index * count, count), count), :]


def dispatch_body(x_ref, code_ref, out_ref):
    core = lax.axis_index("c")
    n = x_ref.shape[0] // 2
    c0, c1, part = row_codes(out_ref.shape[0], 10 * core)
    code = code_ref[...]
    own, other = part_of(x_ref, core, n), part_of(x_ref, 1 - core, n)

    def pick(c):
        hit = c == code[0:1, :]
        for k in range(1, code.shape[0]):
            hit = hit | (c == code[k : k + 1, :])
        return jnp.where(hit, 1.0, 0.0).astype(BF)

    def rows(p, x):
        return jnp.dot(p, x, preferred_element_type=F32)

    p0, p1 = pick(c0), pick(c1)
    out_ref[:, 0:256] = rows(p0, own).astype(BF)
    out_ref[:, 256:512] = rows(p0, other).astype(BF)
    tx, ty = rows(p1, own), rows(p1, other)
    tail = jnp.where(part == 0, tx[:, 0:128], tx[:, 128:256])
    tail2 = jnp.where(part == 2, ty[:, 0:128], ty[:, 128:256])
    out_ref[:, 512:640] = jnp.where(part < 2, tail, tail2).astype(BF)


def stack_body(ga_ref, gb_ref, ua_ref, ub_ref, _, __, out_ref):
    k, half = ga_ref.shape
    out_ref[0:k, 0:half] = ga_ref[...]
    out_ref[k:, 0:half] = gb_ref[...]
    out_ref[0:k, half:] = ua_ref[...]
    out_ref[k:, half:] = ub_ref[...]


def up_body(a_ref, w_ref, out_ref, x_ref, t_ref):
    n = a_ref.shape[0]
    x_ref[0:n, :] = a_ref[:, 0:512]
    t_ref[...] = a_ref[:, 512:640].astype(F32)
    for g in range(4):
        x_ref[n:, g * 128 : (g + 1) * 128] = t_ref[pl.ds(g, n // 4, stride=4), :].astype(BF)

    out_ref[...] = jnp.dot(x_ref[...], w_ref[...], preferred_element_type=F32).astype(BF)


def act_body(p_ref, h_ref):
    rows = p_ref.shape[0] // 8
    half = h_ref.shape[1]

    @pl.loop(0, rows // 8)
    def _(i):
        def total(o):
            t = None
            for d in range(8):
                v = p_ref[pl.ds(pl.multiple_of(d * rows + i * 8, 8), 8), o : o + half]
                t = v.astype(F32) if t is None else t + v.astype(F32)
            return t

        g, u = total(0), total(half)
        h = (g / (1.0 + jnp.exp(-g)) * u).astype(BF)
        for d in range(8):
            h_ref[pl.ds(pl.multiple_of(d * rows + i * 8, 8), 8), :] = h


def down_body(h_ref, w_ref, v_ref, out_ref, t_ref):
    n = out_ref.shape[0]
    for k, m in ((0, w_ref), (1, v_ref)):
        t = jnp.dot(h_ref[...], m[...], preferred_element_type=F32)
        out_ref[:, k * 256 : (k + 1) * 256] = t[0:n].astype(BF)
        for g in range(2):
            t_ref[pl.ds(2 * k + g, n // 4, stride=4), :] = t[n:, g * 128 : (g + 1) * 128]
    out_ref[:, 512:640] = t_ref[...].astype(BF)


def weigh_body(code_ref, w_ref, out_ref):
    code = code_ref[...]
    w = w_ref[...]
    c0, c1, _ = row_codes(out_ref.shape[1], 10 * lax.axis_index("c"))

    def weights(c):
        t = jnp.where(c == code[0:1, :], w[0:1, :], 0.0)
        for k in range(1, code.shape[0]):
            t = t + jnp.where(c == code[k : k + 1, :], w[k : k + 1, :], 0.0)
        return t

    for k, m in enumerate((weights(c0), weights(c1))):
        m = jnp.transpose(m)
        hi = m.astype(BF)
        n = m.shape[0]
        out_ref[2 * k * n : (2 * k + 1) * n, :] = hi
        out_ref[(2 * k + 1) * n : (2 * k + 2) * n, :] = (m - hi.astype(F32)).astype(BF)


def combine_body(r_ref, m_ref, own_ref, send_ref):
    n = own_ref.shape[0]
    head = jnp.dot(m_ref[0 : 2 * n, :], r_ref[:, 0:512], preferred_element_type=F32)
    head = head[0:n] + head[n:]
    rest = r_ref[:, 512:640]
    part = lax.rem(lax.broadcasted_iota(jnp.int32, rest.shape, 0), 4)
    parts = [jnp.where(part == p, rest, 0.0).astype(BF) for p in range(4)]
    tail = jnp.dot(m_ref[2 * n :, :], jnp.concatenate(parts, axis=1), preferred_element_type=F32)
    for k, ref in ((0, own_ref), (1, send_ref)):
        for g in range(2):
            p = 2 * k + g
            s = slice(p * 128, (p + 1) * 128)
            ref[:, g * 128 : (g + 1) * 128] = head[:, s] + tail[0:n, s] + tail[n:, s]


def finish_body(own_ref, sent_ref, res_ref, out_ref):
    other = part_of(sent_ref, 1 - lax.axis_index("c"), own_ref.shape[0])
    out_ref[...] = (res_ref[...].astype(F32) + own_ref[...] + other).astype(BF)


def swap(x):
    return lax.ppermute(x, "c", [(0, 1), (1, 0)])


def share(x):
    return lax.all_gather(x, "c", axis=0, tiled=True)


def spread(x, axes):
    return lax.all_to_all(x, axes, split_axis=0, concat_axis=0, tiled=True)


def shards(tokens_in, residual, w_gate, w_up, w_down, expert_ids, slot_pos, route_weights):
    code, weights = (expert_ids * 64 + slot_pos).T, route_weights.T
    hidden_units = w_gate.shape[2]
    sds = jax.ShapeDtypeStruct
    experts = lax.axis_size(E)
    rows = experts * 10
    chunks = sds((experts * 8, 640), BF)
    gate, up, down = w_gate[0], w_up[0], w_down[0]

    tokens = share(tokens_in)
    outgoing = call(dispatch_body, chunks, tokens, code, name="dispatch")
    mixing = call(
        weigh_body, sds((4 * code.shape[1], experts * 8), BF), code, weights, name="weigh"
    )
    gate_b, up_b, down_b = swap(gate), swap(up), swap(down)
    stacked = call(
        stack_body, sds((2 * gate.shape[0], 2 * hidden_units), BF),
        gate, gate_b, up, up_b, down_b, mixing,
        name="stack",
    )
    arrived = spread(outgoing, LINE)
    partial = call(
        up_body,
        sds((rows, 2 * hidden_units), BF),
        arrived, stacked,
        scratch=[pltpu.VMEM((rows, 512), BF), pltpu.VMEM((experts * 8, 128), F32)],
        name="gate_up",
    )
    parts = spread(partial, R)
    hidden = call(act_body, sds((rows, hidden_units), BF), parts, name="act")
    hidden = spread(hidden, R)
    result = call(
        down_body, chunks, hidden, down, down_b,
        scratch=[pltpu.VMEM((experts * 8, 128), F32)],
        name="down",
    )
    returned = spread(result, LINE)
    half_out = sds(tokens_in.shape, F32)
    own, send = call(combine_body, (half_out, half_out), returned, mixing, name="combine")
    return call(
        finish_body, sds(tokens_in.shape, BF), own, share(send), residual, name="finish"
    )


def solution(mesh):
    fine = Mesh(mesh.devices.reshape(4, 2, 2, 4, 4, 2), T + E)
    in_specs = (
        P(E, T),
        P(E, T),
        P(E, T, None),
        P(E, T, None),
        P(E, None, T),
        P(E, None),
        P(E, None),
        P(E, None),
    )
    return jax.shard_map(
        shards, mesh=fine, in_specs=in_specs, out_specs=P(E, T), check_vma=False
    )
```

```python
import jax
import jax.numpy as jnp
from jax import lax
from jax.experimental import pallas as pl
from jax.experimental.pallas import tpu as pltpu
from jax.sharding import Mesh, PartitionSpec as P

BF = jnp.bfloat16
F32 = jnp.float32
T = ("y", "xh", "c")
R = ("y", "xh")
E = ("z3", "z2", "z1", "z0", "xl")
LINE = ("xl", "z0", "z1", "z3", "z2")
VMEM = pl.BlockSpec(memory_space=pltpu.VMEM)


def call(body, out, *args, name, limit=16 << 20, scratch=()):
    return pl.pallas_call(
        body,
        out_shape=out,
        in_specs=[VMEM] * len(args),
        out_specs=jax.tree.map(lambda _: VMEM, out),
        scratch_shapes=list(scratch),
        compiler_params=pltpu.CompilerParams(vmem_limit_bytes=limit),
        name=name,
    )(*args)


def expert_of(chunk):
    total, left = 0, chunk
    for axis in reversed(LINE):
        size = lax.axis_size(axis)
        stride = lax.axis_size(E[E.index(axis) + 1 :]) if axis != E[-1] else 1
        total = total + lax.rem(left, size) * stride
        left = left // size
    return total


def row_codes(rows, first):
    r = lax.broadcasted_iota(jnp.int32, (rows, 1), 0)
    d, j = r // 8, lax.rem(r, 8)
    base = expert_of(d) * 64 + first
    return base + j, base + 8 + j // 4, lax.rem(j, 4)


def part_of(ref, index, count):
    return ref[pl.ds(pl.multiple_of(index * count, count), count), :]


def dispatch_body(x_ref, code_ref, out_ref):
    core = lax.axis_index("c")
    n = x_ref.shape[0] // 2
    c0, c1, part = row_codes(out_ref.shape[0], 10 * core)
    code = code_ref[...]
    own, other = part_of(x_ref, core, n), part_of(x_ref, 1 - core, n)

    def pick(c):
        hit = c == code[0:1, :]
        for k in range(1, code.shape[0]):
            hit = hit | (c == code[k : k + 1, :])
        return jnp.where(hit, 1.0, 0.0).astype(BF)

    def rows(p, x):
        return jnp.dot(p, x, preferred_element_type=F32)

    p0, p1 = pick(c0), pick(c1)
    out_ref[:, 0:256] = rows(p0, own).astype(BF)
    out_ref[:, 256:512] = rows(p0, other).astype(BF)
    tx, ty = rows(p1, own), rows(p1, other)
    tail = jnp.where(part == 0, tx[:, 0:128], tx[:, 128:256])
    tail2 = jnp.where(part == 2, ty[:, 0:128], ty[:, 128:256])
    out_ref[:, 512:640] = jnp.where(part < 2, tail, tail2).astype(BF)


def stack_body(ga_ref, gb_ref, ua_ref, ub_ref, _, __, out_ref):
    k, half = ga_ref.shape
    out_ref[0:k, 0:half] = ga_ref[...]
    out_ref[k:, 0:half] = gb_ref[...]
    out_ref[0:k, half:] = ua_ref[...]
    out_ref[k:, half:] = ub_ref[...]


def up_body(a_ref, w_ref, out_ref, x_ref, t_ref):
    n = a_ref.shape[0]
    x_ref[0:n, :] = a_ref[:, 0:512]
    t_ref[...] = a_ref[:, 512:640].astype(F32)
    for g in range(4):
        x_ref[n:, g * 128 : (g + 1) * 128] = t_ref[pl.ds(g, n // 4, stride=4), :].astype(BF)

    out_ref[...] = jnp.dot(x_ref[...], w_ref[...], preferred_element_type=F32).astype(BF)


def act_body(p_ref, h_ref):
    rows = p_ref.shape[0] // 8
    half = h_ref.shape[1]

    @pl.loop(0, rows // 8)
    def _(i):
        def total(o):
            t = None
            for d in range(8):
                v = p_ref[pl.ds(pl.multiple_of(d * rows + i * 8, 8), 8), o : o + half]
                t = v.astype(F32) if t is None else t + v.astype(F32)
            return t

        g, u = total(0), total(half)
        h = (g / (1.0 + jnp.exp(-g)) * u).astype(BF)
        for d in range(8):
            h_ref[pl.ds(pl.multiple_of(d * rows + i * 8, 8), 8), :] = h


def down_body(h_ref, w_ref, v_ref, out_ref, t_ref):
    n = out_ref.shape[0]
    for k, m in ((0, w_ref), (1, v_ref)):
        t = jnp.dot(h_ref[...], m[...], preferred_element_type=F32)
        out_ref[:, k * 256 : (k + 1) * 256] = t[0:n].astype(BF)
        for g in range(2):
            t_ref[pl.ds(2 * k + g, n // 4, stride=4), :] = t[n:, g * 128 : (g + 1) * 128]
    out_ref[:, 512:640] = t_ref[...].astype(BF)


def weigh_body(code_ref, w_ref, out_ref):
    code = code_ref[...]
    w = w_ref[...]
    c0, c1, _ = row_codes(out_ref.shape[1], 10 * lax.axis_index("c"))

    def weights(c):
        t = jnp.where(c == code[0:1, :], w[0:1, :], 0.0)
        for k in range(1, code.shape[0]):
            t = t + jnp.where(c == code[k : k + 1, :], w[k : k + 1, :], 0.0)
        return t

    for k, m in enumerate((weights(c0), weights(c1))):
        m = jnp.transpose(m)
        hi = m.astype(BF)
        n = m.shape[0]
        out_ref[2 * k * n : (2 * k + 1) * n, :] = hi
        out_ref[(2 * k + 1) * n : (2 * k + 2) * n, :] = (m - hi.astype(F32)).astype(BF)


def combine_body(r_ref, m_ref, own_ref, send_ref):
    n = own_ref.shape[0]
    head = jnp.dot(m_ref[0 : 2 * n, :], r_ref[:, 0:512], preferred_element_type=F32)
    head = head[0:n] + head[n:]
    rest = r_ref[:, 512:640]
    part = lax.rem(lax.broadcasted_iota(jnp.int32, rest.shape, 0), 4)
    parts = [jnp.where(part == p, rest, 0.0).astype(BF) for p in range(4)]
    tail = jnp.dot(m_ref[2 * n :, :], jnp.concatenate(parts, axis=1), preferred_element_type=F32)
    for k, ref in ((0, own_ref), (1, send_ref)):
        for g in range(2):
            p = 2 * k + g
            s = slice(p * 128, (p + 1) * 128)
            ref[:, g * 128 : (g + 1) * 128] = head[:, s] + tail[0:n, s] + tail[n:, s]


def finish_body(own_ref, sent_ref, res_ref, out_ref):
    other = part_of(sent_ref, 1 - lax.axis_index("c"), own_ref.shape[0])
    out_ref[...] = (res_ref[...].astype(F32) + own_ref[...] + other).astype(BF)


def swap(x):
    return lax.ppermute(x, "c", [(0, 1), (1, 0)])


def share(x):
    return lax.all_gather(x, "c", axis=0, tiled=True)


def spread(x, axes):
    return lax.all_to_all(x, axes, split_axis=0, concat_axis=0, tiled=True)


def shards(tokens_in, residual, w_gate, w_up, w_down, expert_ids, slot_pos, route_weights):
    code, weights = (expert_ids * 64 + slot_pos).T, route_weights.T
    hidden_units = w_gate.shape[2]
    sds = jax.ShapeDtypeStruct
    experts = lax.axis_size(E)
    rows = experts * 10
    chunks = sds((experts * 8, 640), BF)
    gate, up, down = w_gate[0], w_up[0], w_down[0]

    tokens = share(tokens_in)
    outgoing = call(dispatch_body, chunks, tokens, code, name="dispatch")
    mixing = call(
        weigh_body, sds((4 * code.shape[1], experts * 8), BF), code, weights, name="weigh"
    )
    gate_b, up_b, down_b = swap(gate), swap(up), swap(down)
    stacked = call(
        stack_body, sds((2 * gate.shape[0], 2 * hidden_units), BF),
        gate, gate_b, up, up_b, down_b, mixing,
        name="stack",
    )
    arrived = spread(outgoing, LINE)
    partial = call(
        up_body,
        sds((rows, 2 * hidden_units), BF),
        arrived, stacked,
        scratch=[pltpu.VMEM((rows, 512), BF), pltpu.VMEM((experts * 8, 128), F32)],
        name="gate_up",
    )
    parts = spread(partial, R)
    hidden = call(act_body, sds((rows, hidden_units), BF), parts, name="act")
    hidden = spread(hidden, R)
    result = call(
        down_body, chunks, hidden, down, down_b,
        scratch=[pltpu.VMEM((experts * 8, 128), F32)],
        name="down",
    )
    returned = spread(result, LINE)
    half_out = sds(tokens_in.shape, F32)
    own, send = call(combine_body, (half_out, half_out), returned, mixing, name="combine")
    return call(
        finish_body, sds(tokens_in.shape, BF), own, share(send), residual, name="finish"
    )


def solution(mesh):
    fine = Mesh(mesh.devices.reshape(4, 2, 2, 2, 2, 2, 2, 2), T + E)
    in_specs = (
        P(E, T),
        P(E, T),
        P(E, T, None),
        P(E, T, None),
        P(E, None, T),
        P(E, None),
        P(E, None),
        P(E, None),
    )
    return jax.shard_map(
        shards, mesh=fine, in_specs=in_specs, out_specs=P(E, T), check_vma=False
    )
```

```python
import jax
import jax.numpy as jnp
from jax import lax
from jax.experimental import pallas as pl
from jax.experimental.pallas import tpu as pltpu
from jax.sharding import Mesh, PartitionSpec as P

BF = jnp.bfloat16
F32 = jnp.float32
T = ("y", "xh", "c")
R = ("y", "xh")
E = ("z3", "z2", "z1", "z0", "xl")
LINE = ("xl", "z2", "z1", "z0", "z3")
VMEM = pl.BlockSpec(memory_space=pltpu.VMEM)


def call(body, out, *args, name, limit=16 << 20, scratch=()):
    return pl.pallas_call(
        body,
        out_shape=out,
        in_specs=[VMEM] * len(args),
        out_specs=jax.tree.map(lambda _: VMEM, out),
        scratch_shapes=list(scratch),
        compiler_params=pltpu.CompilerParams(vmem_limit_bytes=limit),
        name=name,
    )(*args)


def expert_of(chunk):
    total, left = 0, chunk
    for axis in reversed(LINE):
        size = lax.axis_size(axis)
        stride = lax.axis_size(E[E.index(axis) + 1 :]) if axis != E[-1] else 1
        total = total + lax.rem(left, size) * stride
        left = left // size
    return total


def row_codes(rows, first):
    r = lax.broadcasted_iota(jnp.int32, (rows, 1), 0)
    d, j = r // 8, lax.rem(r, 8)
    base = expert_of(d) * 64 + first
    return base + j, base + 8 + j // 4, lax.rem(j, 4)


def part_of(ref, index, count):
    return ref[pl.ds(pl.multiple_of(index * count, count), count), :]


def dispatch_body(x_ref, code_ref, out_ref):
    core = lax.axis_index("c")
    n = x_ref.shape[0] // 2
    c0, c1, part = row_codes(out_ref.shape[0], 10 * core)
    code = code_ref[...]
    own, other = part_of(x_ref, core, n), part_of(x_ref, 1 - core, n)

    def pick(c):
        hit = c == code[0:1, :]
        for k in range(1, code.shape[0]):
            hit = hit | (c == code[k : k + 1, :])
        return jnp.where(hit, 1.0, 0.0).astype(BF)

    def rows(p, x):
        return jnp.dot(p, x, preferred_element_type=F32)

    p0, p1 = pick(c0), pick(c1)
    out_ref[:, 0:256] = rows(p0, own).astype(BF)
    out_ref[:, 256:512] = rows(p0, other).astype(BF)
    tx, ty = rows(p1, own), rows(p1, other)
    tail = jnp.where(part == 0, tx[:, 0:128], tx[:, 128:256])
    tail2 = jnp.where(part == 2, ty[:, 0:128], ty[:, 128:256])
    out_ref[:, 512:640] = jnp.where(part < 2, tail, tail2).astype(BF)


def stack_body(ga_ref, gb_ref, ua_ref, ub_ref, _, __, out_ref):
    k, half = ga_ref.shape
    out_ref[0:k, 0:half] = ga_ref[...]
    out_ref[k:, 0:half] = gb_ref[...]
    out_ref[0:k, half:] = ua_ref[...]
    out_ref[k:, half:] = ub_ref[...]


def up_body(a_ref, w_ref, out_ref, x_ref, t_ref):
    n = a_ref.shape[0]
    x_ref[0:n, :] = a_ref[:, 0:512]
    t_ref[...] = a_ref[:, 512:640].astype(F32)
    for g in range(4):
        x_ref[n:, g * 128 : (g + 1) * 128] = t_ref[pl.ds(g, n // 4, stride=4), :].astype(BF)

    out_ref[...] = jnp.dot(x_ref[...], w_ref[...], preferred_element_type=F32).astype(BF)


def act_body(p_ref, h_ref):
    rows = p_ref.shape[0] // 8
    half = h_ref.shape[1]

    @pl.loop(0, rows // 8)
    def _(i):
        def total(o):
            t = None
            for d in range(8):
                v = p_ref[pl.ds(pl.multiple_of(d * rows + i * 8, 8), 8), o : o + half]
                t = v.astype(F32) if t is None else t + v.astype(F32)
            return t

        g, u = total(0), total(half)
        h = (g / (1.0 + jnp.exp(-g)) * u).astype(BF)
        for d in range(8):
            h_ref[pl.ds(pl.multiple_of(d * rows + i * 8, 8), 8), :] = h


def down_body(h_ref, w_ref, v_ref, out_ref, t_ref):
    n = out_ref.shape[0]
    for k, m in ((0, w_ref), (1, v_ref)):
        t = jnp.dot(h_ref[...], m[...], preferred_element_type=F32)
        out_ref[:, k * 256 : (k + 1) * 256] = t[0:n].astype(BF)
        for g in range(2):
            t_ref[pl.ds(2 * k + g, n // 4, stride=4), :] = t[n:, g * 128 : (g + 1) * 128]
    out_ref[:, 512:640] = t_ref[...].astype(BF)


def weigh_body(code_ref, w_ref, out_ref):
    code = code_ref[...]
    w = w_ref[...]
    c0, c1, _ = row_codes(out_ref.shape[1], 10 * lax.axis_index("c"))

    def weights(c):
        t = jnp.where(c == code[0:1, :], w[0:1, :], 0.0)
        for k in range(1, code.shape[0]):
            t = t + jnp.where(c == code[k : k + 1, :], w[k : k + 1, :], 0.0)
        return t

    for k, m in enumerate((weights(c0), weights(c1))):
        m = jnp.transpose(m)
        hi = m.astype(BF)
        n = m.shape[0]
        out_ref[2 * k * n : (2 * k + 1) * n, :] = hi
        out_ref[(2 * k + 1) * n : (2 * k + 2) * n, :] = (m - hi.astype(F32)).astype(BF)


def combine_body(r_ref, m_ref, own_ref, send_ref):
    n = own_ref.shape[0]
    head = jnp.dot(m_ref[0 : 2 * n, :], r_ref[:, 0:512], preferred_element_type=F32)
    head = head[0:n] + head[n:]
    rest = r_ref[:, 512:640]
    part = lax.rem(lax.broadcasted_iota(jnp.int32, rest.shape, 0), 4)
    parts = [jnp.where(part == p, rest, 0.0).astype(BF) for p in range(4)]
    tail = jnp.dot(m_ref[2 * n :, :], jnp.concatenate(parts, axis=1), preferred_element_type=F32)
    for k, ref in ((0, own_ref), (1, send_ref)):
        for g in range(2):
            p = 2 * k + g
            s = slice(p * 128, (p + 1) * 128)
            ref[:, g * 128 : (g + 1) * 128] = head[:, s] + tail[0:n, s] + tail[n:, s]


def finish_body(own_ref, sent_ref, res_ref, out_ref):
    other = part_of(sent_ref, 1 - lax.axis_index("c"), own_ref.shape[0])
    out_ref[...] = (res_ref[...].astype(F32) + own_ref[...] + other).astype(BF)


def swap(x):
    return lax.ppermute(x, "c", [(0, 1), (1, 0)])


def share(x):
    return lax.all_gather(x, "c", axis=0, tiled=True)


def spread(x, axes):
    return lax.all_to_all(x, axes, split_axis=0, concat_axis=0, tiled=True)


def shards(tokens_in, residual, w_gate, w_up, w_down, expert_ids, slot_pos, route_weights):
    code, weights = (expert_ids * 64 + slot_pos).T, route_weights.T
    hidden_units = w_gate.shape[2]
    sds = jax.ShapeDtypeStruct
    experts = lax.axis_size(E)
    rows = experts * 10
    chunks = sds((experts * 8, 640), BF)
    gate, up, down = w_gate[0], w_up[0], w_down[0]

    tokens = share(tokens_in)
    outgoing = call(dispatch_body, chunks, tokens, code, name="dispatch")
    mixing = call(
        weigh_body, sds((4 * code.shape[1], experts * 8), BF), code, weights, name="weigh"
    )
    gate_b, up_b, down_b = swap(gate), swap(up), swap(down)
    stacked = call(
        stack_body, sds((2 * gate.shape[0], 2 * hidden_units), BF),
        gate, gate_b, up, up_b, down_b, mixing,
        name="stack",
    )
    arrived = spread(outgoing, LINE)
    partial = call(
        up_body,
        sds((rows, 2 * hidden_units), BF),
        arrived, stacked,
        scratch=[pltpu.VMEM((rows, 512), BF), pltpu.VMEM((experts * 8, 128), F32)],
        name="gate_up",
    )
    parts = spread(partial, R)
    hidden = call(act_body, sds((rows, hidden_units), BF), parts, name="act")
    hidden = spread(hidden, R)
    result = call(
        down_body, chunks, hidden, down, down_b,
        scratch=[pltpu.VMEM((experts * 8, 128), F32)],
        name="down",
    )
    returned = spread(result, LINE)
    half_out = sds(tokens_in.shape, F32)
    own, send = call(combine_body, (half_out, half_out), returned, mixing, name="combine")
    return call(
        finish_body, sds(tokens_in.shape, BF), own, share(send), residual, name="finish"
    )


def solution(mesh):
    fine = Mesh(mesh.devices.reshape(4, 2, 2, 2, 2, 2, 2, 2), T + E)
    in_specs = (
        P(E, T),
        P(E, T),
        P(E, T, None),
        P(E, T, None),
        P(E, None, T),
        P(E, None),
        P(E, None),
        P(E, None),
    )
    return jax.shard_map(
        shards, mesh=fine, in_specs=in_specs, out_specs=P(E, T), check_vma=False
    )
```
